32 devices in a mesh: row: 8 (over z, x), col: 4 (over y, core).
Axes of the slice: x: 2, y: 2, z: 4, core: 2. Of those that a mesh axis runs over, the one named last changes fastest.
Arguments:
- panels_t: float32 [1024, 2048], P('col', 'row'), as said below
- trailing_t: float32 [3072, 2048], P('col', 'row'), may hold values from -0.125 to 0.125
Outputs:
- r_factor: float32 [1024, 1024], P('row', 'col')
- coefficients: float32 [1024, 3072], P('row', 'col')
The draws below stay inside these ranges and needn't reach their ends.
Inputs may be any that keep to these rules, and one draw needn't show every extreme that they name: `panels_t`: panel_matrix has full column rank.
All inputs are finite; a program needn't handle non-finite values.
Results may differ from the reference program's by a relative error of at most 0.0003.
Values sent between devices are 32-bit elements; how exact they have to be, the bound alone decides.
A program may use at most 64 MiB of HBM per device.

```python
import jax
import jax.numpy as jnp
from jax import lax

TRAIL_COLS = 3072
PANEL_COLS = 1024
ROWS = 2048


def draw_panels_t(key, part):
    key_base = jax.random.fold_in(key, 11)
    key_noise = jax.random.fold_in(key_base, 1)
    key_upper = jax.random.fold_in(key_base, 2)
    key_chain = jax.random.fold_in(key_base, 4)
    key_flip = jax.random.fold_in(key_base, 5)
    noise = jnp.clip(jax.random.normal(key_noise, (PANEL_COLS, ROWS), jnp.float32), -6.0, 6.0)
    noise = noise * ROWS ** (-0.5)
    upper_part = jax.random.normal(key_upper, (PANEL_COLS, PANEL_COLS), jnp.float32) * (0.25 * PANEL_COLS ** (-0.5))
    magnitude = jax.random.uniform(key_chain, (PANEL_COLS - 1,), jnp.float32, 0.8, 0.9)
    flips = jnp.where(jax.random.bernoulli(key_flip, 0.5, (PANEL_COLS - 1,)), 1.0, -1.0).astype(jnp.float32)
    chain = jnp.diag(magnitude * flips, 1)
    upper_part = jnp.triu(upper_part, 1) + chain + jnp.eye(PANEL_COLS, dtype=jnp.float32)
    result = jnp.dot(upper_part.T, noise, precision=lax.Precision.HIGHEST)
    return result


def steps_of(key, extent, shards, low, high):
    level = 1.0
    for dim, parts in shards:
        heights = jax.random.uniform(jax.random.fold_in(jax.random.fold_in(key, 6), dim), (parts,), jnp.float32, low / len(shards), high / len(shards))
        level = level * jnp.repeat(jnp.exp(heights), extent[dim] // parts).reshape((-1,) + (1,) * (len(extent) - 1 - dim))
    return level


def scatter_about(own_key, extent, width, reach, split=(), kind=jnp.bfloat16):
    gain = steps_of(own_key, extent, split, -0.22, 0.18) if split else 1.0
    entries = jax.random.normal(own_key, extent, jnp.float32) * width * gain
    return jnp.minimum(jnp.maximum(entries, -reach), reach).astype(kind)


def setup_inputs(seed: int = 0) -> dict:
    key_of = jax.random.split(jax.random.key(seed), 3)
    panels_t = draw_panels_t(jax.random.fold_in(key_of[2], 71), 0)
    trailing_t = scatter_about(key_of[1], (TRAIL_COLS, ROWS), ROWS ** -0.5, 0.125, ((0, 4), (1, 8)), jnp.float32)
    return {"panels_t": panels_t, "trailing_t": trailing_t}


def reference(panels_t, trailing_t):
    highest = lax.Precision.HIGHEST
    factor_q, raw_r = jnp.linalg.qr(panels_t.T)
    signs = jnp.sign(jnp.diagonal(raw_r))
    r_factor = signs[:, None] * raw_r
    top = signs[:, None] * jnp.dot(factor_q.T, trailing_t.T, precision=highest)
    coefficients = jax.scipy.linalg.solve_triangular(r_factor, top, lower=False)
    return (r_factor, coefficients)
```

```python
import jax
import jax.numpy as jnp
from jax import lax
from jax.experimental import pallas as pl
from jax.experimental.pallas import tpu as pltpu
from jax.sharding import PartitionSpec as P

BLOCK = 128
MICRO = 8


def product(left, right):
    return jnp.dot(left, right, precision=lax.Precision.HIGHEST)


def lanes(tile, lane):
    return jnp.broadcast_to(tile[:, lane : lane + 1], tile.shape)


def sublanes(tile, row):
    return jnp.broadcast_to(tile[row : row + 1, :], tile.shape)


def factor_block(square):
    count = BLOCK // MICRO
    shape = (MICRO, BLOCK)
    row_id = lax.broadcasted_iota(jnp.int32, shape, 0)
    lane_id = lax.broadcasted_iota(jnp.int32, shape, 1)
    rest = [square[MICRO * i : MICRO * (i + 1), :] for i in range(count)]
    unit = [jnp.where(row_id + MICRO * i == lane_id, 1.0, 0.0) for i in range(count)]
    upper, inverse = [], []
    for b in range(count):
        base = MICRO * b
        tile, side = rest[b], unit[b]
        cols = [lanes(tile, base + c) for c in range(MICRO)]
        scales, pivots, rows, sides = [], {}, [], []
        upper_tile, side_tile = jnp.zeros(shape, jnp.float32), jnp.zeros(shape, jnp.float32)
        for k in range(MICRO):
            scale = lax.rsqrt(sublanes(cols[k], k))
            below = cols[k] * scale
            row = sublanes(tile, k) * scale
            side_row = sublanes(side, k) * scale
            for c in range(k + 1, MICRO):
                pivots[c, k] = sublanes(below, c)
                cols[c] = cols[c] - below * pivots[c, k]
            tile = tile - below * row
            side = side - below * side_row
            upper_tile = jnp.where(row_id == k, row, upper_tile)
            side_tile = jnp.where(row_id == k, side_row, side_tile)
            scales.append(scale)
            rows.append(row)
            sides.append(side_row)
        upper.append(jnp.where(row_id + base <= lane_id, upper_tile, 0.0))
        inverse.append(jnp.where(row_id + base >= lane_id, side_tile, 0.0))
        for i in range(b + 1, count):
            tile, side = rest[i], unit[i]
            cols = [lanes(tile, base + c) for c in range(MICRO)]
            for k in range(MICRO):
                below = cols[k] * scales[k]
                for c in range(k + 1, MICRO):
                    cols[c] = cols[c] - below * pivots[c, k]
                tile = tile - below * rows[k]
                side = side - below * sides[k]
            rest[i], unit[i] = tile, side
    return jnp.concatenate(upper, axis=0), jnp.concatenate(inverse, axis=0)


def factor_kernel(gram_ref, upper_ref, inverse_ref, work_ref):
    total = gram_ref.shape[0]
    work_ref[...] = gram_ref[...]
    column = lax.broadcasted_iota(jnp.int32, (BLOCK, total), 1)

    @pl.loop(0, total // BLOCK)
    def _(k):
        start = pl.multiple_of(k * BLOCK, BLOCK)
        here = pl.ds(start, BLOCK)
        diagonal, inverse = factor_block(work_ref[here, here])
        panel = product(inverse, work_ref[here, :])
        work_ref[here, :] = panel
        work_ref[here, here] = inverse
        upper_ref[here, :] = jnp.where(column >= start + BLOCK, panel, 0.0)
        upper_ref[here, here] = diagonal
        inverse_ref[here, :] = jnp.where(column < start, panel, 0.0)
        inverse_ref[here, here] = inverse

        @pl.loop(k + 1, total // BLOCK)
        def _(i):
            there = pl.ds(pl.multiple_of(i * BLOCK, BLOCK), BLOCK)
            work_ref[there, here] = jnp.zeros((BLOCK, BLOCK), jnp.float32)
            work_ref[there, :] -= lax.dot_general(
                work_ref[here, there],
                work_ref[here, :],
                (((0,), (0,)), ((), ())),
                precision=lax.Precision.HIGHEST,
                preferred_element_type=jnp.float32,
            )


def factor(gram):
    total = gram.shape[0]
    whole = jax.ShapeDtypeStruct(gram.shape, jnp.float32)
    return pl.pallas_call(
        factor_kernel,
        out_shape=(whole, whole),
        in_specs=[pl.BlockSpec(memory_space=pltpu.VMEM)],
        out_specs=(pl.BlockSpec(memory_space=pltpu.VMEM),) * 2,
        scratch_shapes=[pltpu.VMEM(gram.shape, jnp.float32)],
        compiler_params=pltpu.CompilerParams(vmem_limit_bytes=32 * 1024 * 1024),
        cost_estimate=pl.CostEstimate(flops=60 * total**3, bytes_accessed=12 * total**2, transcendentals=0),
    )(gram)


def local(panels_t, trailing_t):
    panel = lax.all_gather(panels_t, "col", axis=0, tiled=True)
    gram_part = lax.psum_scatter(product(panels_t, panel.T), "row", scatter_dimension=0, tiled=True)
    gram = lax.all_gather(gram_part, ("col", "row"), axis=0, tiled=True)
    cross = lax.psum_scatter(product(trailing_t, panel.T), "row", scatter_dimension=0, tiled=True)
    r_full, invert = factor(gram)
    slab = product(product(cross, invert.T), invert)
    spread = lax.all_to_all(slab, "row", split_axis=1, concat_axis=0, tiled=True)
    total = r_full.shape[0]
    rows_out = total // lax.axis_size("row")
    cols_out = total // lax.axis_size("col")
    row_start = lax.axis_index("row") * rows_out
    col_start = lax.axis_index("col") * cols_out
    r_block = lax.dynamic_slice(r_full, (row_start, col_start), (rows_out, cols_out))
    return (r_block, spread.T)


def solution(mesh):
    placed = (P("col", "row"), P("col", "row"))
    return jax.shard_map(
        local,
        mesh=mesh,
        in_specs=placed,
        out_specs=(P("row", "col"), P("row", "col")),
        check_vma=False,
    )
```

```python
import jax
import jax.numpy as jnp
from jax import lax
from jax.experimental import pallas as pl
from jax.experimental.pallas import tpu as pltpu
from jax.sharding import PartitionSpec as P

BLOCK = 128
MICRO = 8
MESH = pl.DeviceIdType.MESH


def product(left, right):
    return jnp.dot(left, right, precision=lax.Precision.HIGHEST)


def lanes(tile, lane):
    return jnp.broadcast_to(tile[:, lane : lane + 1], tile.shape)


def sublanes(tile, row):
    return jnp.broadcast_to(tile[row : row + 1, :], tile.shape)


def factor_block(square):
    count = BLOCK // MICRO
    shape = (MICRO, BLOCK)
    row_id = lax.broadcasted_iota(jnp.int32, shape, 0)
    lane_id = lax.broadcasted_iota(jnp.int32, shape, 1)
    rest = [square[MICRO * i : MICRO * (i + 1), :] for i in range(count)]
    unit = [jnp.where(row_id + MICRO * i == lane_id, 1.0, 0.0) for i in range(count)]
    upper, inverse = [], []
    for b in range(count):
        base = MICRO * b
        tile, side = rest[b], unit[b]
        cols = [lanes(tile, base + c) for c in range(MICRO)]
        scales, pivots, rows, sides = [], {}, [], []
        upper_tile, side_tile = jnp.zeros(shape, jnp.float32), jnp.zeros(shape, jnp.float32)
        for k in range(MICRO):
            scale = lax.rsqrt(sublanes(cols[k], k))
            below = cols[k] * scale
            row = sublanes(tile, k) * scale
            side_row = sublanes(side, k) * scale
            for c in range(k + 1, MICRO):
                pivots[c, k] = sublanes(below, c)
                cols[c] = cols[c] - below * pivots[c, k]
            tile = tile - below * row
            side = side - below * side_row
            upper_tile = jnp.where(row_id == k, row, upper_tile)
            side_tile = jnp.where(row_id == k, side_row, side_tile)
            scales.append(scale)
            rows.append(row)
            sides.append(side_row)
        upper.append(jnp.where(row_id + base <= lane_id, upper_tile, 0.0))
        inverse.append(jnp.where(row_id + base >= lane_id, side_tile, 0.0))
        for i in range(b + 1, count):
            tile, side = rest[i], unit[i]
            cols = [lanes(tile, base + c) for c in range(MICRO)]
            for k in range(MICRO):
                below = cols[k] * scales[k]
                for c in range(k + 1, MICRO):
                    cols[c] = cols[c] - below * pivots[c, k]
                tile = tile - below * rows[k]
                side = side - below * sides[k]
            rest[i], unit[i] = tile, side
    return jnp.concatenate(upper, axis=0), jnp.concatenate(inverse, axis=0)


def unstack(stacked_ref, work_ref, width):
    count = stacked_ref.shape[0] // width
    for i in range(count):
        for j in range(i, count):
            if j - i <= count // 2:
                held = stacked_ref[pl.ds(i * width, width), pl.ds((j - i) * width, width)]
            else:
                held = stacked_ref[pl.ds(j * width, width), pl.ds((count + i - j) * width, width)].T
            work_ref[pl.ds(i * width, width), pl.ds(j * width, width)] = held
            if j > i:
                work_ref[pl.ds(j * width, width), pl.ds(i * width, width)] = jnp.zeros((width, width), jnp.float32)


def factor_kernel(width, gram_ref, upper_ref, inverse_ref, work_ref):
    total = gram_ref.shape[0]
    if width is None:
        work_ref[...] = gram_ref[...]
    else:
        unstack(gram_ref, work_ref, width)
    column = lax.broadcasted_iota(jnp.int32, (BLOCK, total), 1)

    @pl.loop(0, total // BLOCK)
    def _(k):
        start = pl.multiple_of(k * BLOCK, BLOCK)
        here = pl.ds(start, BLOCK)
        diagonal, inverse = factor_block(work_ref[here, here])
        panel = product(inverse, work_ref[here, :])
        work_ref[here, :] = panel
        work_ref[here, here] = inverse
        upper_ref[here, :] = jnp.where(column >= start + BLOCK, panel, 0.0)
        upper_ref[here, here] = diagonal
        inverse_ref[here, :] = jnp.where(column < start, panel, 0.0)
        inverse_ref[here, here] = inverse

        @pl.loop(k + 1, total // BLOCK)
        def _(i):
            there = pl.ds(pl.multiple_of(i * BLOCK, BLOCK), BLOCK)
            work_ref[there, here] = jnp.zeros((BLOCK, BLOCK), jnp.float32)
            work_ref[there, :] -= lax.dot_general(
                work_ref[here, there],
                work_ref[here, :],
                (((0,), (0,)), ((), ())),
                precision=lax.Precision.HIGHEST,
                preferred_element_type=jnp.float32,
            )


def factor(gram, width):
    total = gram.shape[0]
    whole = jax.ShapeDtypeStruct((total, total), jnp.float32)
    return pl.pallas_call(
        lambda *refs: factor_kernel(width, *refs),
        out_shape=(whole, whole),
        in_specs=[pl.BlockSpec(memory_space=pltpu.VMEM)],
        out_specs=(pl.BlockSpec(memory_space=pltpu.VMEM),) * 2,
        scratch_shapes=[pltpu.VMEM((total, total), jnp.float32)],
        compiler_params=pltpu.CompilerParams(vmem_limit_bytes=32 * 1024 * 1024),
        cost_estimate=pl.CostEstimate(flops=60 * total**3, bytes_accessed=12 * total**2, transcendentals=0),
    )(gram)


def remote(source, target, send, receive, row, col):
    return pltpu.make_async_remote_copy(
        src_ref=source,
        dst_ref=target,
        send_sem=send,
        recv_sem=receive,
        device_id=(row, col),
        device_id_type=MESH,
    )


def greet(peers):
    barrier = pltpu.get_barrier_semaphore()
    for row, col in peers:
        pl.semaphore_signal(barrier, inc=1, device_id=(row, col), device_id_type=MESH)
    pl.semaphore_wait(barrier, len(peers))


def column_peers(cols):
    row, col = lax.axis_index("row"), lax.axis_index("col")
    mate = col + 1 - 2 * lax.rem(col, 2)
    return [(row, lax.rem(col + 2 * t, cols)) for t in range(1, cols // 2)] + [(row, mate)]


def gather_columns(cols, pieces, ready, view, sems):
    line_send, line_recv, mate_send, mate_recv = sems
    row, col = lax.axis_index("row"), lax.axis_index("col")
    mate = col + 1 - 2 * lax.rem(col, 2)
    half = cols // 2
    sent = []

    def launch(copy):
        copy.start()
        sent.append(copy)

    def to_mate(source, owner, s, t):
        launch(remote(source, view(owner, s), mate_send.at[s, t], mate_recv.at[s, t], row, mate))

    def relay(s):
        for t in range(1, half):
            owner = lax.rem(col - 2 * t + cols, cols)
            place = view(owner, s)
            remote(place, place, line_send.at[s, t], line_recv.at[s, t], row, mate).wait_recv()
            to_mate(place, owner, s, t)

    for s in range(pieces):
        source = ready(s)
        for t in range(1, half):
            peer = lax.rem(col + 2 * t, cols)
            launch(remote(source, view(col, s), line_send.at[s, t], line_recv.at[s, t], row, peer))
        to_mate(source, col, s, 0)
        if s > 0:
            relay(s - 1)
    relay(pieces - 1)
    for s in range(pieces):
        for t in range(half):
            place = view(lax.rem(mate - 2 * t + cols, cols), s)
            remote(place, place, mate_send.at[s, t], mate_recv.at[s, t], row, mate).wait_recv()
    for copy in sent:
        copy.wait_send()


def panel_kernel(cols, pieces, block_ref, out_ref, *sems):
    col = lax.axis_index("col")
    greet(column_peers(cols))
    rows = block_ref.shape[0] // pieces

    def part(s):
        return pl.ds(s * rows, rows)

    gather_columns(cols, pieces, lambda s: block_ref.at[part(s)], lambda c, s: out_ref.at[c, part(s)], sems)
    out_ref[col] = block_ref[...]


def column_sems(cols, pieces):
    return [pltpu.SemaphoreType.DMA((pieces, cols // 2))] * 4


def gather_panel(block, cols):
    pieces = 2
    vmem = pl.BlockSpec(memory_space=pltpu.VMEM)
    return pl.pallas_call(
        lambda *refs: panel_kernel(cols, pieces, *refs),
        out_shape=jax.ShapeDtypeStruct((cols,) + block.shape, jnp.float32),
        in_specs=[vmem],
        out_specs=vmem,
        scratch_shapes=column_sems(cols, pieces),
        compiler_params=pltpu.CompilerParams(collective_id=0, has_side_effects=True, vmem_limit_bytes=16 * 1024 * 1024),
    )(block)


def gram_kernel(rows, cols, part_ref, out_ref, land_ref, sum_send, sum_recv, row_send, row_recv, *sems):
    row, col = lax.axis_index("row"), lax.axis_index("col")
    peers = [(lax.rem(row + s, rows), col) for s in range(1, rows)]
    greet(peers + column_peers(cols))
    sent = []
    for s in range(1, rows):
        peer = lax.rem(row + s, rows)
        copy = remote(part_ref.at[peer], land_ref.at[s], sum_send.at[s], sum_recv.at[s], peer, col)
        copy.start()
        sent.append(copy)
    total = part_ref[row]
    for s in range(1, rows):
        sent[s - 1].wait_recv()
        total = total + land_ref[s]
    out_ref[col, row] = total

    def view(c, s):
        return out_ref.at[c, lax.rem(row - s + rows, rows)]

    for s in range(1, rows):
        peer = lax.rem(row + s, rows)
        copy = remote(view(col, 0), view(col, 0), row_send.at[s], row_recv.at[s], peer, col)
        copy.start()
        sent.append(copy)

    def ready(s):
        if s > 0:
            place = view(col, s)
            remote(place, place, row_send.at[s], row_recv.at[s], lax.rem(row + s, rows), col).wait_recv()
        return view(col, s)

    gather_columns(cols, rows, ready, view, sems)
    for copy in sent:
        copy.wait_send()


def gather_gram(part, cols):
    rows = part.shape[0]
    vmem = pl.BlockSpec(memory_space=pltpu.VMEM)
    return pl.pallas_call(
        lambda *refs: gram_kernel(rows, cols, *refs),
        out_shape=jax.ShapeDtypeStruct((cols,) + part.shape, jnp.float32),
        in_specs=[vmem],
        out_specs=vmem,
        scratch_shapes=[pltpu.VMEM(part.shape, jnp.float32)] + [pltpu.SemaphoreType.DMA((rows,))] * 4 + column_sems(cols, rows),
        compiler_params=pltpu.CompilerParams(collective_id=1, has_side_effects=True, vmem_limit_bytes=24 * 1024 * 1024),
        cost_estimate=pl.CostEstimate(flops=10**11, bytes_accessed=8 * cols * part.size, transcendentals=0),
    )(part)


def spread_kernel(rows, slab_ref, out_ref, send, receive):
    row, col = lax.axis_index("row"), lax.axis_index("col")
    greet([(lax.rem(row + s, rows), col) for s in range(1, rows)])
    sent = []
    for s in range(1, rows):
        peer = lax.rem(row + s, rows)
        copy = remote(slab_ref.at[peer], out_ref.at[row], send.at[s], receive.at[s], peer, col)
        copy.start()
        sent.append(copy)
    out_ref[row] = slab_ref[row]
    for s in range(1, rows):
        place = out_ref.at[lax.rem(row - s + rows, rows)]
        remote(place, place, send.at[s], receive.at[s], lax.rem(row + s, rows), col).wait_recv()
    for copy in sent:
        copy.wait_send()


def spread_slab(slab):
    rows = slab.shape[0]
    vmem = pl.BlockSpec(memory_space=pltpu.VMEM)
    return pl.pallas_call(
        lambda *refs: spread_kernel(rows, *refs),
        out_shape=jax.ShapeDtypeStruct(slab.shape, jnp.float32),
        in_specs=[vmem],
        out_specs=vmem,
        scratch_shapes=[pltpu.SemaphoreType.DMA((rows,))] * 2,
        compiler_params=pltpu.CompilerParams(collective_id=2, has_side_effects=True, vmem_limit_bytes=8 * 1024 * 1024),
    )(slab)


def direct(panels_t, trailing_t, rows, cols):
    width, depth = panels_t.shape
    total = width * cols
    near = cols // 2 + 1
    panel = gather_panel(panels_t, cols).reshape(total, depth)
    turned = jnp.concatenate([panel, panel])
    ring = lax.dynamic_slice_in_dim(turned, lax.axis_index("col") * width, near * width, 0)
    part = product(panels_t, ring.T).reshape(rows, width // rows, near * width)
    cross = lax.psum_scatter(product(trailing_t, panel.T), "row", scatter_dimension=0, tiled=True)
    stacked = gather_gram(part, cols).reshape(total, near * width)
    r_full, invert = factor(stacked, width)
    slab = product(product(cross, invert.T), invert)
    slab = slab.reshape(slab.shape[0], rows, total // rows).transpose(1, 0, 2)
    spread = spread_slab(slab)
    return r_full, spread.transpose(2, 0, 1).reshape(total // rows, -1)


def plain(panels_t, trailing_t):
    panel = lax.all_gather(panels_t, "col", axis=0, tiled=True)
    gram_part = lax.psum_scatter(product(panels_t, panel.T), "row", scatter_dimension=0, tiled=True)
    gram = lax.all_gather(gram_part, ("col", "row"), axis=0, tiled=True)
    cross = lax.psum_scatter(product(trailing_t, panel.T), "row", scatter_dimension=0, tiled=True)
    r_full, invert = factor(gram, None)
    slab = product(product(cross, invert.T), invert)
    return r_full, lax.all_to_all(slab, "row", split_axis=1, concat_axis=0, tiled=True).T


def local(panels_t, trailing_t):
    rows, cols = lax.axis_size("row"), lax.axis_size("col")
    width = panels_t.shape[0]
    if width % BLOCK == 0 and width // rows % MICRO == 0 and cols % 2 == 0:
        r_full, coef_block = direct(panels_t, trailing_t, rows, cols)
    else:
        r_full, coef_block = plain(panels_t, trailing_t)
    total = r_full.shape[0]
    rows_out = total // rows
    cols_out = total // cols
    row_start = lax.axis_index("row") * rows_out
    col_start = lax.axis_index("col") * cols_out
    r_block = lax.dynamic_slice(r_full, (row_start, col_start), (rows_out, cols_out))
    return (r_block, coef_block)


def solution(mesh):
    placed = (P("col", "row"), P("col", "row"))
    return jax.shard_map(
        local,
        mesh=mesh,
        in_specs=placed,
        out_specs=(P("row", "col"), P("row", "col")),
        check_vma=False,
    )
```

```python
import jax
import jax.numpy as jnp
from jax import lax
from jax.experimental import pallas as pl
from jax.experimental.pallas import tpu as pltpu
from jax.sharding import PartitionSpec as P

BLOCK = 128
MICRO = 8
MESH = pl.DeviceIdType.MESH


def product(left, right):
    return jnp.dot(left, right, precision=lax.Precision.HIGHEST)


def contract(left, right, left_dim, right_dim):
    return lax.dot_general(
        left,
        right,
        (((left_dim,), (right_dim,)), ((), ())),
        precision=lax.Precision.HIGHEST,
        preferred_element_type=jnp.float32,
    )


def lanes(tile, lane):
    return jnp.broadcast_to(tile[:, lane : lane + 1], tile.shape)


def sublanes(tile, row):
    return jnp.broadcast_to(tile[row : row + 1, :], tile.shape)


def factor_block(square):
    count = BLOCK // MICRO
    shape = (MICRO, BLOCK)
    row_id = lax.broadcasted_iota(jnp.int32, shape, 0)
    lane_id = lax.broadcasted_iota(jnp.int32, shape, 1)
    rest = [square[MICRO * i : MICRO * (i + 1), :] for i in range(count)]
    unit = [jnp.where(row_id + MICRO * i == lane_id, 1.0, 0.0) for i in range(count)]
    upper, inverse = [], []
    for b in range(count):
        base = MICRO * b
        tile, side = rest[b], unit[b]
        cols = [lanes(tile, base + c) for c in range(MICRO)]
        scales, pivots, rows, sides = [], {}, [], []
        upper_tile, side_tile = jnp.zeros(shape, jnp.float32), jnp.zeros(shape, jnp.float32)
        for k in range(MICRO):
            scale = lax.rsqrt(sublanes(cols[k], k))
            below = cols[k] * scale
            row = sublanes(tile, k) * scale
            side_row = sublanes(side, k) * scale
            for c in range(k + 1, MICRO):
                pivots[c, k] = sublanes(below, c)
                cols[c] = cols[c] - below * pivots[c, k]
            tile = tile - below * row
            side = side - below * side_row
            upper_tile = jnp.where(row_id == k, row, upper_tile)
            side_tile = jnp.where(row_id == k, side_row, side_tile)
            scales.append(scale)
            rows.append(row)
            sides.append(side_row)
        upper.append(jnp.where(row_id + base <= lane_id, upper_tile, 0.0))
        inverse.append(jnp.where(row_id + base >= lane_id, side_tile, 0.0))
        for i in range(b + 1, count):
            tile, side = rest[i], unit[i]
            cols = [lanes(tile, base + c) for c in range(MICRO)]
            for k in range(MICRO):
                below = cols[k] * scales[k]
                for c in range(k + 1, MICRO):
                    cols[c] = cols[c] - below * pivots[c, k]
                tile = tile - below * rows[k]
                side = side - below * sides[k]
            rest[i], unit[i] = tile, side
    return jnp.concatenate(upper, axis=0), jnp.concatenate(inverse, axis=0)


def unstack(stacked_ref, work_ref, width):
    count = stacked_ref.shape[0]

    def block(i, step):
        return stacked_ref[i, :, :, pl.ds(step * width, width)].reshape(width, width)

    for i in range(count):
        for j in range(i, count):
            held = block(i, j - i) if j - i <= count // 2 else block(j, count + i - j).T
            work_ref[pl.ds(i * width, width), pl.ds(j * width, width)] = held
            if j > i:
                work_ref[pl.ds(j * width, width), pl.ds(i * width, width)] = jnp.zeros((width, width), jnp.float32)


def factor_loop(upper_ref, inverse_ref, work_ref, beside):
    total = work_ref.shape[0]
    column = lax.broadcasted_iota(jnp.int32, (BLOCK, total), 1)

    @pl.loop(0, total // BLOCK)
    def _(k):
        beside(k)
        start = pl.multiple_of(k * BLOCK, BLOCK)
        here = pl.ds(start, BLOCK)
        diagonal, inverse = factor_block(work_ref[here, here])
        panel = product(inverse, work_ref[here, :])
        work_ref[here, :] = panel
        work_ref[here, here] = inverse
        upper_ref[here, :] = jnp.where(column >= start + BLOCK, panel, 0.0)
        upper_ref[here, here] = diagonal
        inverse_ref[here, :] = jnp.where(column < start, panel, 0.0)
        inverse_ref[here, here] = inverse

        @pl.loop(k + 1, total // BLOCK)
        def _(i):
            there = pl.ds(pl.multiple_of(i * BLOCK, BLOCK), BLOCK)
            work_ref[there, here] = jnp.zeros((BLOCK, BLOCK), jnp.float32)
            work_ref[there, :] -= contract(work_ref[here, there], work_ref[here, :], 0, 0)


def factor_kernel(gram_ref, upper_ref, inverse_ref, work_ref):
    work_ref[...] = gram_ref[...]
    factor_loop(upper_ref, inverse_ref, work_ref, lambda k: None)


def factor(gram):
    total = gram.shape[0]
    whole = jax.ShapeDtypeStruct((total, total), jnp.float32)
    return pl.pallas_call(
        factor_kernel,
        out_shape=(whole, whole),
        in_specs=[pl.BlockSpec(memory_space=pltpu.VMEM)],
        out_specs=(pl.BlockSpec(memory_space=pltpu.VMEM),) * 2,
        scratch_shapes=[pltpu.VMEM((total, total), jnp.float32)],
        compiler_params=pltpu.CompilerParams(vmem_limit_bytes=32 * 1024 * 1024),
        cost_estimate=pl.CostEstimate(flops=60 * total**3, bytes_accessed=12 * total**2, transcendentals=0),
    )(gram)


def remote(source, target, send, receive, row, col):
    return pltpu.make_async_remote_copy(
        src_ref=source,
        dst_ref=target,
        send_sem=send,
        recv_sem=receive,
        device_id=(row, col),
        device_id_type=MESH,
    )


def greet(peers):
    barrier = pltpu.get_barrier_semaphore()
    for row, col in peers:
        pl.semaphore_signal(barrier, inc=1, device_id=(row, col), device_id_type=MESH)
    pl.semaphore_wait(barrier, len(peers))


def column_peers(cols):
    row, col = lax.axis_index("row"), lax.axis_index("col")
    mate = col + 1 - 2 * lax.rem(col, 2)
    return [(row, lax.rem(col + 2 * t, cols)) for t in range(1, cols // 2)] + [(row, mate)]


def gather_columns(cols, pieces, ready, view, sems):
    line_send, line_recv, mate_send, mate_recv = sems
    row, col = lax.axis_index("row"), lax.axis_index("col")
    mate = col + 1 - 2 * lax.rem(col, 2)
    half = cols // 2
    sent = []

    def launch(copy):
        copy.start()
        sent.append(copy)

    def to_mate(source, owner, s, t):
        launch(remote(source, view(owner, s), mate_send.at[s, t], mate_recv.at[s, t], row, mate))

    def relay(s):
        for t in range(1, half):
            owner = lax.rem(col - 2 * t + cols, cols)
            place = view(owner, s)
            remote(place, place, line_send.at[s, t], line_recv.at[s, t], row, mate).wait_recv()
            to_mate(place, owner, s, t)

    for s in range(pieces):
        source = ready(s)
        for t in range(1, half):
            peer = lax.rem(col + 2 * t, cols)
            launch(remote(source, view(col, s), line_send.at[s, t], line_recv.at[s, t], row, peer))
        to_mate(source, col, s, 0)
        if s > 0:
            relay(s - 1)
    relay(pieces - 1)
    for s in range(pieces):
        for t in range(half):
            place = view(lax.rem(mate - 2 * t + cols, cols), s)
            remote(place, place, mate_send.at[s, t], mate_recv.at[s, t], row, mate).wait_recv()
    for copy in sent:
        copy.wait_send()


def panel_kernel(cols, pieces, block_ref, out_ref, *sems):
    col = lax.axis_index("col")
    greet(column_peers(cols))
    rows = block_ref.shape[0] // pieces

    def part(s):
        return pl.ds(s * rows, rows)

    gather_columns(cols, pieces, lambda s: block_ref.at[part(s)], lambda c, s: out_ref.at[c, part(s)], sems)
    out_ref[col] = block_ref[...]


def column_sems(cols, pieces):
    return [pltpu.SemaphoreType.DMA((pieces, cols // 2))] * 4


def gather_panel(block, cols):
    pieces = 2
    vmem = pl.BlockSpec(memory_space=pltpu.VMEM)
    return pl.pallas_call(
        lambda *refs: panel_kernel(cols, pieces, *refs),
        out_shape=jax.ShapeDtypeStruct((cols,) + block.shape, jnp.float32),
        in_specs=[vmem],
        out_specs=vmem,
        scratch_shapes=column_sems(cols, pieces),
        compiler_params=pltpu.CompilerParams(collective_id=0, has_side_effects=True, vmem_limit_bytes=16 * 1024 * 1024),
    )(block)


def reduce_gram(rows, cols, part_ref, out_ref, land_ref, sums, gathers, column, between):
    row, col = lax.axis_index("row"), lax.axis_index("col")
    sum_send, sum_recv = sums
    row_send, row_recv = gathers
    sent = []
    for s in range(1, rows):
        peer = lax.rem(row + s, rows)
        copy = remote(part_ref.at[peer], land_ref.at[s], sum_send.at[s], sum_recv.at[s], peer, col)
        copy.start()
        sent.append(copy)
    between()
    total = part_ref[row]
    for s in range(1, rows):
        sent[s - 1].wait_recv()
        total = total + land_ref[s]
    out_ref[col, row] = total

    def view(c, s):
        return out_ref.at[c, lax.rem(row - s + rows, rows)]

    for s in range(1, rows):
        peer = lax.rem(row + s, rows)
        copy = remote(view(col, 0), view(col, 0), row_send.at[s], row_recv.at[s], peer, col)
        copy.start()
        sent.append(copy)

    def ready(s):
        if s > 0:
            place = view(col, s)
            remote(place, place, row_send.at[s], row_recv.at[s], lax.rem(row + s, rows), col).wait_recv()
        return view(col, s)

    gather_columns(cols, rows, ready, view, column)
    for copy in sent:
        copy.wait_send()


def solve(cross_ref, row, inverse_ref, middle_ref, slab_ref):
    total = inverse_ref.shape[0]
    step = 2 * BLOCK
    for j in range(0, total, step):
        stop = j + step
        middle_ref[:, j:stop] = contract(cross_ref[row, :, :stop], inverse_ref[j:stop, :stop], 1, 1)
    wide = total // slab_ref.shape[0]
    for j in range(0, total, step):
        found = contract(middle_ref[:, j:], inverse_ref[j:, j : j + step], 1, 0)
        for t in range(0, step, wide):
            slab_ref[(j + t) // wide] = found[:, t : t + wide]


def spread_slab(rows, slab_ref, out_ref, send, receive):
    row, col = lax.axis_index("row"), lax.axis_index("col")
    sent = []
    for s in range(1, rows):
        peer = lax.rem(row + s, rows)
        copy = remote(slab_ref.at[peer], out_ref.at[row], send.at[s], receive.at[s], peer, col)
        copy.start()
        sent.append(copy)
    out_ref[row] = slab_ref[row]
    for s in range(1, rows):
        place = out_ref.at[lax.rem(row - s + rows, rows)]
        remote(place, place, send.at[s], receive.at[s], lax.rem(row + s, rows), col).wait_recv()
    for copy in sent:
        copy.wait_send()


def main_kernel(rows, cols, width, *refs):
    part_ref, trailing_ref, panel_ref, upper_out, coef_out = refs[:5]
    stacked_ref, land_ref, cross_ref, pair_ref, line_ref, work_ref, upper_ref, inverse_ref, middle_ref, slab_ref = refs[5:15]
    sums, gathers, spreads, pairs, lines = (refs[15 + 2 * i : 17 + 2 * i] for i in range(5))
    column = refs[25:]
    row, col = lax.axis_index("row"), lax.axis_index("col")
    half = rows // 2
    place, side = row // 2, lax.rem(row, 2)
    greet([(lax.rem(row + s, rows), col) for s in range(1, rows)] + column_peers(cols))

    def multiply():
        @pl.loop(0, rows)
        def _(r):
            cross_ref[r] = contract(trailing_ref[r], panel_ref[...], 1, 1)

    reduce_gram(rows, cols, part_ref, stacked_ref, land_ref, sums, gathers, column, multiply)

    def target(s, which):
        return 2 * lax.rem(place + s, half) + which

    def pair_copy(s):
        mate = 2 * place + 1 - side
        return remote(cross_ref.at[target(s, 1 - side)], pair_ref.at[s], pairs[0].at[s], pairs[1].at[s], mate, col)

    def line_copy(s):
        owner = target(s, side)
        return remote(cross_ref.at[owner], line_ref.at[s], lines[0].at[s], lines[1].at[s], owner, col)

    def fold(s):
        pair_copy(s).wait_recv()
        cross_ref[target(s, side)] += pair_ref[s]
        if s > 0:
            line_copy(s).start()

    for s in list(range(1, half)) + [0]:
        pair_copy(s).start()
    unstack(stacked_ref, work_ref, width)

    def beside(k):
        for s in range(1, half):
            pl.when(k == s + 1)(lambda s=s: fold(s))

    factor_loop(upper_ref, inverse_ref, work_ref, beside)
    upper_out[...] = upper_ref[
        pl.ds(pl.multiple_of(row * upper_out.shape[0], MICRO), upper_out.shape[0]),
        pl.ds(pl.multiple_of(col * upper_out.shape[1], BLOCK), upper_out.shape[1]),
    ]
    fold(0)
    for s in range(1, half):
        line_copy(s).wait_recv()
        cross_ref[row] += line_ref[s]
    solve(cross_ref, row, inverse_ref, middle_ref, slab_ref)
    spread_slab(rows, slab_ref, coef_out, *spreads)
    for s in range(half):
        pair_copy(s).wait_send()
        if s > 0:
            line_copy(s).wait_send()


def direct(panels_t, trailing_t, rows, cols):
    width, depth = panels_t.shape
    total = width * cols
    near = cols // 2 + 1
    panel = gather_panel(panels_t, cols).reshape(total, depth)
    turned = jnp.concatenate([panel, panel])
    ring = lax.dynamic_slice_in_dim(turned, lax.axis_index("col") * width, near * width, 0)
    part = product(panels_t, ring.T).reshape(rows, width // rows, near * width)
    trailing = trailing_t.reshape(rows, -1, depth)
    thick = trailing.shape[1]
    vmem = pl.BlockSpec(memory_space=pltpu.VMEM)
    shapes = [
        (cols,) + part.shape,
        part.shape,
        (rows, thick, total),
        (rows // 2, thick, total),
        (rows // 2, thick, total),
        (total, total),
        (total, total),
        (total, total),
        (thick, total),
        (rows, thick, total // rows),
    ]
    semaphores = [pltpu.SemaphoreType.DMA((rows,))] * 6 + [pltpu.SemaphoreType.DMA((rows // 2,))] * 4
    r_block, spread = pl.pallas_call(
        lambda *refs: main_kernel(rows, cols, width, *refs),
        out_shape=(
            jax.ShapeDtypeStruct((total // rows, total // cols), jnp.float32),
            jax.ShapeDtypeStruct((rows, thick, total // rows), jnp.float32),
        ),
        in_specs=[vmem] * 3,
        out_specs=(vmem, vmem),
        scratch_shapes=[pltpu.VMEM(shape, jnp.float32) for shape in shapes] + semaphores + column_sems(cols, rows),
        compiler_params=pltpu.CompilerParams(collective_id=1, has_side_effects=True, vmem_limit_bytes=48 * 1024 * 1024),
    )(part, trailing, panel)
    return r_block, spread.transpose(2, 0, 1).reshape(total // rows, -1)


def plain(panels_t, trailing_t):
    panel = lax.all_gather(panels_t, "col", axis=0, tiled=True)
    gram_part = lax.psum_scatter(product(panels_t, panel.T), "row", scatter_dimension=0, tiled=True)
    gram = lax.all_gather(gram_part, ("col", "row"), axis=0, tiled=True)
    cross = lax.psum_scatter(product(trailing_t, panel.T), "row", scatter_dimension=0, tiled=True)
    r_full, invert = factor(gram)
    slab = product(product(cross, invert.T), invert)
    return r_full, lax.all_to_all(slab, "row", split_axis=1, concat_axis=0, tiled=True).T


def local(panels_t, trailing_t):
    rows, cols = lax.axis_size("row"), lax.axis_size("col")
    width = panels_t.shape[0]
    total = width * cols
    thick = trailing_t.shape[0] // rows
    tiled = width % BLOCK == 0 and total // rows % BLOCK == 0 and width // rows % MICRO == 0 and thick % MICRO == 0
    if tiled and rows % 2 == 0 and cols % 2 == 0 and rows // 2 < total // BLOCK:
        return direct(panels_t, trailing_t, rows, cols)
    r_full, coef_block = plain(panels_t, trailing_t)
    rows_out = total // rows
    row_start = lax.axis_index("row") * rows_out
    col_start = lax.axis_index("col") * width
    r_block = lax.dynamic_slice(r_full, (row_start, col_start), (rows_out, width))
    return (r_block, coef_block)


def solution(mesh):
    placed = (P("col", "row"), P("col", "row"))
    return jax.shard_map(
        local,
        mesh=mesh,
        in_specs=placed,
        out_specs=(P("row", "col"), P("row", "col")),
        check_vma=False,
    )
```

```python
import jax
import jax.numpy as jnp
from jax import lax
from jax.experimental import pallas as pl
from jax.experimental.pallas import tpu as pltpu
from jax.sharding import PartitionSpec as P

BLOCK = 128
MICRO = 8
MESH = pl.DeviceIdType.MESH


def product(left, right):
    return jnp.dot(left, right, precision=lax.Precision.HIGHEST)


def contract(left, right, left_dim, right_dim):
    return lax.dot_general(
        left,
        right,
        (((left_dim,), (right_dim,)), ((), ())),
        precision=lax.Precision.HIGHEST,
        preferred_element_type=jnp.float32,
    )


def lanes(tile, lane):
    return jnp.broadcast_to(tile[:, lane : lane + 1], tile.shape)


def sublanes(tile, row):
    return jnp.broadcast_to(tile[row : row + 1, :], tile.shape)


def factor_block(square):
    count = BLOCK // MICRO
    shape = (MICRO, BLOCK)
    row_id = lax.broadcasted_iota(jnp.int32, shape, 0)
    lane_id = lax.broadcasted_iota(jnp.int32, shape, 1)
    rest = [square[MICRO * i : MICRO * (i + 1), :] for i in range(count)]
    unit = [jnp.where(row_id + MICRO * i == lane_id, 1.0, 0.0) for i in range(count)]
    upper, inverse = [], []
    for b in range(count):
        base = MICRO * b
        tile, side = rest[b], unit[b]
        cols = [lanes(tile, base + c) for c in range(MICRO)]
        scales, pivots, rows, sides = [], {}, [], []
        upper_tile, side_tile = jnp.zeros(shape, jnp.float32), jnp.zeros(shape, jnp.float32)
        for k in range(MICRO):
            scale = lax.rsqrt(sublanes(cols[k], k))
            below = cols[k] * scale
            row = sublanes(tile, k) * scale
            side_row = sublanes(side, k) * scale
            for c in range(k + 1, MICRO):
                pivots[c, k] = sublanes(below, c)
                cols[c] = cols[c] - below * pivots[c, k]
            tile = tile - below * row
            side = side - below * side_row
            upper_tile = jnp.where(row_id == k, row, upper_tile)
            side_tile = jnp.where(row_id == k, side_row, side_tile)
            scales.append(scale)
            rows.append(row)
            sides.append(side_row)
        upper.append(jnp.where(row_id + base <= lane_id, upper_tile, 0.0))
        inverse.append(jnp.where(row_id + base >= lane_id, side_tile, 0.0))
        for i in range(b + 1, count):
            tile, side = rest[i], unit[i]
            cols = [lanes(tile, base + c) for c in range(MICRO)]
            for k in range(MICRO):
                below = cols[k] * scales[k]
                for c in range(k + 1, MICRO):
                    cols[c] = cols[c] - below * pivots[c, k]
                tile = tile - below * rows[k]
                side = side - below * sides[k]
            rest[i], unit[i] = tile, side
    return jnp.concatenate(upper, axis=0), jnp.concatenate(inverse, axis=0)


def unstack(stacked_ref, work_ref, width):
    count = stacked_ref.shape[0]

    def block(i, step):
        return stacked_ref[i, :, :, pl.ds(step * width, width)].reshape(width, width)

    for i in range(count):
        for j in range(i, count):
            held = block(i, j - i) if j - i <= count // 2 else block(j, count + i - j).T
            work_ref[pl.ds(i * width, width), pl.ds(j * width, width)] = held
            if j > i:
                work_ref[pl.ds(j * width, width), pl.ds(i * width, width)] = jnp.zeros((width, width), jnp.float32)


def factor_loop(upper_ref, inverse_ref, work_ref, beside):
    total = work_ref.shape[0]
    column = lax.broadcasted_iota(jnp.int32, (BLOCK, total), 1)

    @pl.loop(0, total // BLOCK)
    def _(k):
        beside(k)
        start = pl.multiple_of(k * BLOCK, BLOCK)
        here = pl.ds(start, BLOCK)
        diagonal, inverse = factor_block(work_ref[here, here])
        panel = product(inverse, work_ref[here, :])
        work_ref[here, :] = panel
        work_ref[here, here] = inverse
        upper_ref[here, :] = jnp.where(column >= start + BLOCK, panel, 0.0)
        upper_ref[here, here] = diagonal
        inverse_ref[here, :] = jnp.where(column < start, panel, 0.0)
        inverse_ref[here, here] = inverse

        @pl.loop(k + 1, total // BLOCK)
        def _(i):
            there = pl.ds(pl.multiple_of(i * BLOCK, BLOCK), BLOCK)
            work_ref[there, here] = jnp.zeros((BLOCK, BLOCK), jnp.float32)
            work_ref[there, :] -= contract(work_ref[here, there], work_ref[here, :], 0, 0)


def factor_kernel(gram_ref, upper_ref, inverse_ref, work_ref):
    work_ref[...] = gram_ref[...]
    factor_loop(upper_ref, inverse_ref, work_ref, lambda k: None)


def factor(gram):
    total = gram.shape[0]
    whole = jax.ShapeDtypeStruct((total, total), jnp.float32)
    return pl.pallas_call(
        factor_kernel,
        out_shape=(whole, whole),
        in_specs=[pl.BlockSpec(memory_space=pltpu.VMEM)],
        out_specs=(pl.BlockSpec(memory_space=pltpu.VMEM),) * 2,
        scratch_shapes=[pltpu.VMEM((total, total), jnp.float32)],
        compiler_params=pltpu.CompilerParams(vmem_limit_bytes=32 * 1024 * 1024),
        cost_estimate=pl.CostEstimate(flops=60 * total**3, bytes_accessed=12 * total**2, transcendentals=0),
    )(gram)


def remote(source, target, send, receive, row, col):
    return pltpu.make_async_remote_copy(
        src_ref=source,
        dst_ref=target,
        send_sem=send,
        recv_sem=receive,
        device_id=(row, col),
        device_id_type=MESH,
    )


def greet(peers):
    barrier = pltpu.get_barrier_semaphore()
    for row, col in peers:
        pl.semaphore_signal(barrier, inc=1, device_id=(row, col), device_id_type=MESH)
    pl.semaphore_wait(barrier, len(peers))


def column_peers(cols):
    row, col = lax.axis_index("row"), lax.axis_index("col")
    mate = col + 1 - 2 * lax.rem(col, 2)
    return [(row, lax.rem(col + 2 * t, cols)) for t in range(1, cols // 2)] + [(row, mate)]


def gather_columns(cols, pieces, ready, view, sems):
    line_send, line_recv, mate_send, mate_recv = sems
    row, col = lax.axis_index("row"), lax.axis_index("col")
    mate = col + 1 - 2 * lax.rem(col, 2)
    half = cols // 2
    sent = []

    def launch(copy):
        copy.start()
        sent.append(copy)

    def to_mate(source, owner, s, t):
        launch(remote(source, view(owner, s), mate_send.at[s, t], mate_recv.at[s, t], row, mate))

    def relay(s):
        for t in range(1, half):
            owner = lax.rem(col - 2 * t + cols, cols)
            place = view(owner, s)
            remote(place, place, line_send.at[s, t], line_recv.at[s, t], row, mate).wait_recv()
            to_mate(place, owner, s, t)

    for s in range(pieces):
        source = ready(s)
        for t in range(1, half):
            peer = lax.rem(col + 2 * t, cols)
            launch(remote(source, view(col, s), line_send.at[s, t], line_recv.at[s, t], row, peer))
        to_mate(source, col, s, 0)
        if s > 0:
            relay(s - 1)
    relay(pieces - 1)
    for s in range(pieces):
        for t in range(half):
            place = view(lax.rem(mate - 2 * t + cols, cols), s)
            remote(place, place, mate_send.at[s, t], mate_recv.at[s, t], row, mate).wait_recv()
    for copy in sent:
        copy.wait_send()


def column_sems(cols, pieces):
    return [pltpu.SemaphoreType.DMA((pieces, cols // 2))] * 4


def gather_panel(cols, block_ref, panel_ref, sems):
    pieces = sems[0].shape[0]
    size = block_ref.shape[0] // pieces

    def part(s):
        return pl.ds(s * size, size)

    gather_columns(cols, pieces, lambda s: block_ref.at[part(s)], lambda c, s: panel_ref.at[c, part(s)], sems)
    panel_ref[lax.axis_index("col")] = block_ref[...]


class Reduction:
    def __init__(self, rows, buffer_ref, pair_ref, line_ref, pairs, lines):
        self.buffer, self.pair, self.line = buffer_ref, pair_ref, line_ref
        self.pairs, self.lines = pairs, lines
        self.row, self.col = lax.axis_index("row"), lax.axis_index("col")
        self.half = rows // 2
        self.place, self.side = self.row // 2, lax.rem(self.row, 2)

    def target(self, s, which):
        return 2 * lax.rem(self.place + s, self.half) + which

    def pair_copy(self, s):
        mate = 2 * self.place + 1 - self.side
        source = self.buffer.at[self.target(s, 1 - self.side)]
        return remote(source, self.pair.at[s], self.pairs[0].at[s], self.pairs[1].at[s], mate, self.col)

    def line_copy(self, s):
        owner = self.target(s, self.side)
        source = self.buffer.at[owner]
        return remote(source, self.line.at[s], self.lines[0].at[s], self.lines[1].at[s], owner, self.col)

    def start(self):
        for s in list(range(1, self.half)) + [0]:
            self.pair_copy(s).start()

    def fold(self, s):
        self.pair_copy(s).wait_recv()
        self.buffer[self.target(s, self.side)] += self.pair[s]
        if s > 0:
            self.line_copy(s).start()

    def finish(self):
        self.fold(0)
        total = self.buffer[self.row]
        for s in range(1, self.half):
            self.line_copy(s).wait_recv()
            total = total + self.line[s]
        return total

    def drain(self):
        for s in range(self.half):
            self.pair_copy(s).wait_send()
            if s > 0:
                self.line_copy(s).wait_send()


def reduce_gram(rows, cols, reduction, out_ref, gathers, column, between):
    row, col = lax.axis_index("row"), lax.axis_index("col")
    row_send, row_recv = gathers
    reduction.start()
    for s in range(1, rows // 2):
        reduction.fold(s)
    between()
    sent = []
    total = reduction.finish()
    out_ref[col, row] = total

    def view(c, s):
        return out_ref.at[c, lax.rem(row - s + rows, rows)]

    for s in range(1, rows):
        peer = lax.rem(row + s, rows)
        copy = remote(view(col, 0), view(col, 0), row_send.at[s], row_recv.at[s], peer, col)
        copy.start()
        sent.append(copy)

    def ready(s):
        if s > 0:
            place = view(col, s)
            remote(place, place, row_send.at[s], row_recv.at[s], lax.rem(row + s, rows), col).wait_recv()
        return view(col, s)

    gather_columns(cols, rows, ready, view, column)
    for copy in sent:
        copy.wait_send()
    reduction.drain()


def solve(cross_ref, inverse_ref, middle_ref, slab_ref):
    total = inverse_ref.shape[0]
    step = 2 * BLOCK
    for j in range(0, total, step):
        stop = j + step
        middle_ref[:, j:stop] = contract(cross_ref[:, :stop], inverse_ref[j:stop, :stop], 1, 1)
    wide = total // slab_ref.shape[0]
    for j in range(0, total, step):
        found = contract(middle_ref[:, j:], inverse_ref[j:, j : j + step], 1, 0)
        for t in range(0, step, wide):
            slab_ref[(j + t) // wide] = found[:, t : t + wide]


def spread_slab(rows, slab_ref, out_ref, send, receive):
    row, col = lax.axis_index("row"), lax.axis_index("col")
    sent = []
    for s in range(1, rows):
        peer = lax.rem(row + s, rows)
        copy = remote(slab_ref.at[peer], out_ref.at[row], send.at[s], receive.at[s], peer, col)
        copy.start()
        sent.append(copy)
    out_ref[row] = slab_ref[row]
    for s in range(1, rows):
        place = out_ref.at[lax.rem(row - s + rows, rows)]
        remote(place, place, send.at[s], receive.at[s], lax.rem(row + s, rows), col).wait_recv()
    for copy in sent:
        copy.wait_send()


def main_kernel(rows, cols, width, *refs):
    block_ref, trailing_ref, upper_out, coef_out = refs[:4]
    panel_ref, part_ref, near_pair_ref, near_line_ref, stacked_ref = refs[4:9]
    cross_ref, pair_ref, line_ref, work_ref, upper_ref, inverse_ref, summed_ref, middle_ref, slab_ref = refs[9:18]
    gathers, spreads, near_pairs, near_lines, pairs, lines = (refs[18 + 2 * i : 20 + 2 * i] for i in range(6))
    first, column = refs[30:34], refs[34:38]
    row, col = lax.axis_index("row"), lax.axis_index("col")
    greet([(lax.rem(row + s, rows), col) for s in range(1, rows)] + column_peers(cols))
    gather_panel(cols, block_ref, panel_ref, first)
    for step in range(cols // 2 + 1):
        held = contract(block_ref[...], panel_ref[lax.rem(col + step, cols)], 1, 1)
        part_ref[:, :, step * width : (step + 1) * width] = held.reshape(rows, width // rows, width)

    def multiply():
        panel = panel_ref[...].reshape(width * cols, panel_ref.shape[2])

        @pl.loop(0, rows)
        def _(r):
            cross_ref[r] = contract(trailing_ref[r], panel, 1, 1)

    near = Reduction(rows, part_ref, near_pair_ref, near_line_ref, near_pairs, near_lines)
    reduce_gram(rows, cols, near, stacked_ref, gathers, column, multiply)
    wide = Reduction(rows, cross_ref, pair_ref, line_ref, pairs, lines)
    wide.start()
    unstack(stacked_ref, work_ref, width)

    def beside(k):
        for s in range(1, rows // 2):
            pl.when(k == s + 1)(lambda s=s: wide.fold(s))

    factor_loop(upper_ref, inverse_ref, work_ref, beside)
    upper_out[...] = upper_ref[
        pl.ds(pl.multiple_of(row * upper_out.shape[0], MICRO), upper_out.shape[0]),
        pl.ds(pl.multiple_of(col * upper_out.shape[1], BLOCK), upper_out.shape[1]),
    ]
    summed_ref[...] = wide.finish()
    solve(summed_ref, inverse_ref, middle_ref, slab_ref)
    spread_slab(rows, slab_ref, coef_out, *spreads)
    wide.drain()


def direct(panels_t, trailing_t, rows, cols):
    width, depth = panels_t.shape
    total = width * cols
    half = rows // 2
    trailing = trailing_t.reshape(rows, -1, depth)
    thick = trailing.shape[1]
    near = (width // rows, (cols // 2 + 1) * width)
    vmem = pl.BlockSpec(memory_space=pltpu.VMEM)
    shapes = [
        (cols, width, depth),
        (rows,) + near,
        (half,) + near,
        (half,) + near,
        (cols, rows) + near,
        (rows, thick, total),
        (half, thick, total),
        (half, thick, total),
        (total, total),
        (total, total),
        (total, total),
        (thick, total),
        (thick, total),
        (rows, thick, total // rows),
    ]
    semaphores = [pltpu.SemaphoreType.DMA((rows,))] * 4 + [pltpu.SemaphoreType.DMA((half,))] * 8
    r_block, spread = pl.pallas_call(
        lambda *refs: main_kernel(rows, cols, width, *refs),
        out_shape=(
            jax.ShapeDtypeStruct((total // rows, total // cols), jnp.float32),
            jax.ShapeDtypeStruct((rows, thick, total // rows), jnp.float32),
        ),
        in_specs=[vmem] * 2,
        out_specs=(vmem, vmem),
        scratch_shapes=[pltpu.VMEM(shape, jnp.float32) for shape in shapes]
        + semaphores
        + column_sems(cols, 2)
        + column_sems(cols, rows),
        compiler_params=pltpu.CompilerParams(collective_id=1, has_side_effects=True, vmem_limit_bytes=48 * 1024 * 1024),
    )(panels_t, trailing)
    return r_block, spread.transpose(2, 0, 1).reshape(total // rows, -1)


def plain(panels_t, trailing_t):
    panel = lax.all_gather(panels_t, "col", axis=0, tiled=True)
    gram_part = lax.psum_scatter(product(panels_t, panel.T), "row", scatter_dimension=0, tiled=True)
    gram = lax.all_gather(gram_part, ("col", "row"), axis=0, tiled=True)
    cross = lax.psum_scatter(product(trailing_t, panel.T), "row", scatter_dimension=0, tiled=True)
    r_full, invert = factor(gram)
    slab = product(product(cross, invert.T), invert)
    return r_full, lax.all_to_all(slab, "row", split_axis=1, concat_axis=0, tiled=True).T


def local(panels_t, trailing_t):
    rows, cols = lax.axis_size("row"), lax.axis_size("col")
    width = panels_t.shape[0]
    total = width * cols
    thick = trailing_t.shape[0] // rows
    tiled = width % BLOCK == 0 and total // rows % BLOCK == 0 and width // rows % MICRO == 0 and thick % MICRO == 0
    if tiled and rows % 2 == 0 and cols % 2 == 0 and rows // 2 < total // BLOCK:
        return direct(panels_t, trailing_t, rows, cols)
    r_full, coef_block = plain(panels_t, trailing_t)
    rows_out = total // rows
    row_start = lax.axis_index("row") * rows_out
    col_start = lax.axis_index("col") * width
    r_block = lax.dynamic_slice(r_full, (row_start, col_start), (rows_out, width))
    return (r_block, coef_block)


def solution(mesh):
    placed = (P("col", "row"), P("col", "row"))
    return jax.shard_map(
        local,
        mesh=mesh,
        in_specs=placed,
        out_specs=(P("row", "col"), P("row", "col")),
        check_vma=False,
    )
```

```python
import jax
import jax.numpy as jnp
from jax import lax
from jax.experimental import pallas as pl
from jax.experimental.pallas import tpu as pltpu
from jax.sharding import PartitionSpec as P

BLOCK = 128
MICRO = 8
MESH = pl.DeviceIdType.MESH


def product(left, right):
    return jnp.dot(left, right, precision=lax.Precision.HIGHEST)


def contract(left, right, left_dim, right_dim):
    return lax.dot_general(
        left,
        right,
        (((left_dim,), (right_dim,)), ((), ())),
        precision=lax.Precision.HIGHEST,
        preferred_element_type=jnp.float32,
    )


def lanes(tile, lane):
    return jnp.broadcast_to(tile[:, lane : lane + 1], tile.shape)


def sublanes(tile, row):
    return jnp.broadcast_to(tile[row : row + 1, :], tile.shape)


def factor_block(square):
    count = BLOCK // MICRO
    shape = (MICRO, BLOCK)
    row_id = lax.broadcasted_iota(jnp.int32, shape, 0)
    lane_id = lax.broadcasted_iota(jnp.int32, shape, 1)
    rest = [square[MICRO * i : MICRO * (i + 1), :] for i in range(count)]
    unit = [jnp.where(row_id + MICRO * i == lane_id, 1.0, 0.0) for i in range(count)]
    upper, inverse = [], []
    for b in range(count):
        base = MICRO * b
        tile, side = rest[b], unit[b]
        cols = [lanes(tile, base + c) for c in range(MICRO)]
        scales, pivots, rows, sides = [], {}, [], []
        upper_tile, side_tile = jnp.zeros(shape, jnp.float32), jnp.zeros(shape, jnp.float32)
        for k in range(MICRO):
            scale = lax.rsqrt(sublanes(cols[k], k))
            below = cols[k] * scale
            row = sublanes(tile, k) * scale
            side_row = sublanes(side, k) * scale
            for c in range(k + 1, MICRO):
                pivots[c, k] = sublanes(below, c)
                cols[c] = cols[c] - below * pivots[c, k]
            tile = tile - below * row
            side = side - below * side_row
            upper_tile = jnp.where(row_id == k, row, upper_tile)
            side_tile = jnp.where(row_id == k, side_row, side_tile)
            scales.append(scale)
            rows.append(row)
            sides.append(side_row)
        upper.append(jnp.where(row_id + base <= lane_id, upper_tile, 0.0))
        inverse.append(jnp.where(row_id + base >= lane_id, side_tile, 0.0))
        for i in range(b + 1, count):
            tile, side = rest[i], unit[i]
            cols = [lanes(tile, base + c) for c in range(MICRO)]
            for k in range(MICRO):
                below = cols[k] * scales[k]
                for c in range(k + 1, MICRO):
                    cols[c] = cols[c] - below * pivots[c, k]
                tile = tile - below * rows[k]
                side = side - below * sides[k]
            rest[i], unit[i] = tile, side
    return jnp.concatenate(upper, axis=0), jnp.concatenate(inverse, axis=0)


def unstack(stacked_ref, work_ref, width):
    count = stacked_ref.shape[0]

    def block(i, step):
        return stacked_ref[i, :, :, pl.ds(step * width, width)].reshape(width, width)

    for i in range(count):
        for j in range(i, count):
            held = block(i, j - i) if j - i <= count // 2 else block(j, count + i - j).T
            work_ref[pl.ds(i * width, width), pl.ds(j * width, width)] = held
            if j > i:
                work_ref[pl.ds(j * width, width), pl.ds(i * width, width)] = jnp.zeros((width, width), jnp.float32)


def factor_loop(upper_ref, inverse_ref, work_ref, beside):
    total = work_ref.shape[0]
    column = lax.broadcasted_iota(jnp.int32, (BLOCK, total), 1)

    @pl.loop(0, total // BLOCK)
    def _(k):
        beside(k)
        start = pl.multiple_of(k * BLOCK, BLOCK)
        here = pl.ds(start, BLOCK)
        diagonal, inverse = factor_block(work_ref[here, here])
        panel = product(inverse, work_ref[here, :])
        work_ref[here, :] = panel
        work_ref[here, here] = inverse
        upper_ref[here, :] = jnp.where(column >= start + BLOCK, panel, 0.0)
        upper_ref[here, here] = diagonal
        inverse_ref[here, :] = jnp.where(column < start, panel, 0.0)
        inverse_ref[here, here] = inverse

        @pl.loop(k + 1, total // BLOCK)
        def _(i):
            there = pl.ds(pl.multiple_of(i * BLOCK, BLOCK), BLOCK)
            work_ref[there, here] = jnp.zeros((BLOCK, BLOCK), jnp.float32)
            work_ref[there, :] -= contract(work_ref[here, there], work_ref[here, :], 0, 0)


def factor_kernel(gram_ref, upper_ref, inverse_ref, work_ref):
    work_ref[...] = gram_ref[...]
    factor_loop(upper_ref, inverse_ref, work_ref, lambda k: None)


def factor(gram):
    total = gram.shape[0]
    whole = jax.ShapeDtypeStruct((total, total), jnp.float32)
    return pl.pallas_call(
        factor_kernel,
        out_shape=(whole, whole),
        in_specs=[pl.BlockSpec(memory_space=pltpu.VMEM)],
        out_specs=(pl.BlockSpec(memory_space=pltpu.VMEM),) * 2,
        scratch_shapes=[pltpu.VMEM((total, total), jnp.float32)],
        compiler_params=pltpu.CompilerParams(vmem_limit_bytes=32 * 1024 * 1024),
        cost_estimate=pl.CostEstimate(flops=60 * total**3, bytes_accessed=12 * total**2, transcendentals=0),
    )(gram)


def remote(source, target, send, receive, row, col):
    return pltpu.make_async_remote_copy(
        src_ref=source,
        dst_ref=target,
        send_sem=send,
        recv_sem=receive,
        device_id=(row, col),
        device_id_type=MESH,
    )


def greet(peers):
    barrier = pltpu.get_barrier_semaphore()
    for row, col in peers:
        pl.semaphore_signal(barrier, inc=1, device_id=(row, col), device_id_type=MESH)
    pl.semaphore_wait(barrier, len(peers))


def column_peers(cols):
    row, col = lax.axis_index("row"), lax.axis_index("col")
    mate = col + 1 - 2 * lax.rem(col, 2)
    return [(row, lax.rem(col + 2 * t, cols)) for t in range(1, cols // 2)] + [(row, mate)]


def gather_columns(cols, pieces, ready, view, sems):
    line_send, line_recv, mate_send, mate_recv = sems
    row, col = lax.axis_index("row"), lax.axis_index("col")
    mate = col + 1 - 2 * lax.rem(col, 2)
    half = cols // 2
    sent = []

    def launch(copy):
        copy.start()
        sent.append(copy)

    def to_mate(source, owner, s, t):
        launch(remote(source, view(owner, s), mate_send.at[s, t], mate_recv.at[s, t], row, mate))

    def relay(s):
        for t in range(1, half):
            owner = lax.rem(col - 2 * t + cols, cols)
            place = view(owner, s)
            remote(place, place, line_send.at[s, t], line_recv.at[s, t], row, mate).wait_recv()
            to_mate(place, owner, s, t)

    for s in range(pieces):
        source = ready(s)
        for t in range(1, half):
            peer = lax.rem(col + 2 * t, cols)
            launch(remote(source, view(col, s), line_send.at[s, t], line_recv.at[s, t], row, peer))
        to_mate(source, col, s, 0)
        if s > 0:
            relay(s - 1)
    relay(pieces - 1)
    for s in range(pieces):
        for t in range(half):
            place = view(lax.rem(mate - 2 * t + cols, cols), s)
            remote(place, place, mate_send.at[s, t], mate_recv.at[s, t], row, mate).wait_recv()
    for copy in sent:
        copy.wait_send()


def column_sems(cols, pieces):
    return [pltpu.SemaphoreType.DMA((pieces, cols // 2))] * 4


def gather_panel(cols, block_ref, panel_ref, sems):
    pieces = sems[0].shape[0]
    size = block_ref.shape[0] // pieces

    def part(s):
        return pl.ds(s * size, size)

    gather_columns(cols, pieces, lambda s: block_ref.at[part(s)], lambda c, s: panel_ref.at[c, part(s)], sems)
    panel_ref[lax.axis_index("col")] = block_ref[...]


class Reduction:
    def __init__(self, rows, buffer_ref, pair_ref, line_ref, pairs, lines):
        self.buffer, self.pair, self.line = buffer_ref, pair_ref, line_ref
        self.pairs, self.lines = pairs, lines
        self.row, self.col = lax.axis_index("row"), lax.axis_index("col")
        self.half = rows // 2
        self.place, self.side = self.row // 2, lax.rem(self.row, 2)

    def target(self, s, which):
        return 2 * lax.rem(self.place + s, self.half) + which

    def pair_copy(self, s):
        mate = 2 * self.place + 1 - self.side
        source = self.buffer.at[self.target(s, 1 - self.side)]
        return remote(source, self.pair.at[s], self.pairs[0].at[s], self.pairs[1].at[s], mate, self.col)

    def line_copy(self, s):
        owner = self.target(s, self.side)
        source = self.buffer.at[owner]
        return remote(source, self.line.at[s], self.lines[0].at[s], self.lines[1].at[s], owner, self.col)

    def start(self):
        for s in list(range(1, self.half)) + [0]:
            self.pair_copy(s).start()

    def fold(self, s):
        self.pair_copy(s).wait_recv()
        self.buffer[self.target(s, self.side)] += self.pair[s]
        if s > 0:
            self.line_copy(s).start()

    def finish(self):
        self.fold(0)
        total = self.buffer[self.row]
        for s in range(1, self.half):
            self.line_copy(s).wait_recv()
            total = total + self.line[s]
        return total

    def drain(self):
        for s in range(self.half):
            self.pair_copy(s).wait_send()
            if s > 0:
                self.line_copy(s).wait_send()


def reduce_gram(rows, cols, reduction, out_ref, gathers, column, between):
    row, col = lax.axis_index("row"), lax.axis_index("col")
    row_send, row_recv = gathers
    reduction.start()
    for s in range(1, rows // 2):
        reduction.fold(s)
    between()
    sent = []
    total = reduction.finish()
    out_ref[col, row] = total

    def view(c, s):
        return out_ref.at[c, lax.rem(row - s + rows, rows)]

    for s in range(1, rows):
        peer = lax.rem(row + s, rows)
        copy = remote(view(col, 0), view(col, 0), row_send.at[s], row_recv.at[s], peer, col)
        copy.start()
        sent.append(copy)

    def ready(s):
        if s > 0:
            place = view(col, s)
            remote(place, place, row_send.at[s], row_recv.at[s], lax.rem(row + s, rows), col).wait_recv()
        return view(col, s)

    gather_columns(cols, rows, ready, view, column)
    for copy in sent:
        copy.wait_send()
    reduction.drain()


def solve(rows, cross_ref, inverse_ref, middle_ref, slab_ref, out_ref, send, receive):
    row, col = lax.axis_index("row"), lax.axis_index("col")
    total = inverse_ref.shape[0]
    step = 2 * BLOCK
    for j in range(0, total, step):
        stop = j + step
        middle_ref[:, j:stop] = contract(cross_ref[:, :stop], inverse_ref[j:stop, :stop], 1, 1)
    wide = total // rows

    def copy_to(peer):
        s = lax.rem(peer - row + rows, rows)
        return remote(slab_ref.at[peer], out_ref.at[row], send.at[s], receive.at[s], peer, col)

    for j in range(total - step, -1, -step):
        found = contract(middle_ref[:, j:], inverse_ref[j:, j : j + step], 1, 0)
        for t in range(0, step, wide):
            peer = (j + t) // wide
            slab_ref[peer] = found[:, t : t + wide]
            pl.when(row != peer)(lambda peer=peer: copy_to(peer).start())
    out_ref[row] = slab_ref[row]
    for s in range(1, rows):
        place = out_ref.at[lax.rem(row - s + rows, rows)]
        remote(place, place, send.at[s], receive.at[s], lax.rem(row + s, rows), col).wait_recv()
    for s in range(1, rows):
        copy_to(lax.rem(row + s, rows)).wait_send()


def main_kernel(rows, cols, width, *refs):
    block_ref, trailing_ref, upper_out, coef_out = refs[:4]
    panel_ref, part_ref, near_pair_ref, near_line_ref, stacked_ref = refs[4:9]
    cross_ref, pair_ref, line_ref, work_ref, upper_ref, inverse_ref, summed_ref, middle_ref, slab_ref = refs[9:18]
    gathers, spreads, near_pairs, near_lines, pairs, lines = (refs[18 + 2 * i : 20 + 2 * i] for i in range(6))
    first, column = refs[30:34], refs[34:38]
    row, col = lax.axis_index("row"), lax.axis_index("col")
    greet([(lax.rem(row + s, rows), col) for s in range(1, rows)] + column_peers(cols))
    gather_panel(cols, block_ref, panel_ref, first)
    for step in range(cols // 2 + 1):
        held = contract(block_ref[...], panel_ref[lax.rem(col + step, cols)], 1, 1)
        part_ref[:, :, step * width : (step + 1) * width] = held.reshape(rows, width // rows, width)

    def multiply():
        panel = panel_ref[...].reshape(width * cols, panel_ref.shape[2])

        @pl.loop(0, rows)
        def _(r):
            cross_ref[r] = contract(trailing_ref[r], panel, 1, 1)

    near = Reduction(rows, part_ref, near_pair_ref, near_line_ref, near_pairs, near_lines)
    reduce_gram(rows, cols, near, stacked_ref, gathers, column, multiply)
    wide = Reduction(rows, cross_ref, pair_ref, line_ref, pairs, lines)
    wide.start()
    unstack(stacked_ref, work_ref, width)

    def beside(k):
        for s in range(1, rows // 2):
            pl.when(k == s + 1)(lambda s=s: wide.fold(s))

    factor_loop(upper_ref, inverse_ref, work_ref, beside)
    upper_out[...] = upper_ref[
        pl.ds(pl.multiple_of(row * upper_out.shape[0], MICRO), upper_out.shape[0]),
        pl.ds(pl.multiple_of(col * upper_out.shape[1], BLOCK), upper_out.shape[1]),
    ]
    summed_ref[...] = wide.finish()
    solve(rows, summed_ref, inverse_ref, middle_ref, slab_ref, coef_out, *spreads)
    wide.drain()


def direct(panels_t, trailing_t, rows, cols):
    width, depth = panels_t.shape
    total = width * cols
    half = rows // 2
    trailing = trailing_t.reshape(rows, -1, depth)
    thick = trailing.shape[1]
    near = (width // rows, (cols // 2 + 1) * width)
    vmem = pl.BlockSpec(memory_space=pltpu.VMEM)
    shapes = [
        (cols, width, depth),
        (rows,) + near,
        (half,) + near,
        (half,) + near,
        (cols, rows) + near,
        (rows, thick, total),
        (half, thick, total),
        (half, thick, total),
        (total, total),
        (total, total),
        (total, total),
        (thick, total),
        (thick, total),
        (rows, thick, total // rows),
    ]
    semaphores = [pltpu.SemaphoreType.DMA((rows,))] * 4 + [pltpu.SemaphoreType.DMA((half,))] * 8
    r_block, spread = pl.pallas_call(
        lambda *refs: main_kernel(rows, cols, width, *refs),
        out_shape=(
            jax.ShapeDtypeStruct((total // rows, total // cols), jnp.float32),
            jax.ShapeDtypeStruct((rows, thick, total // rows), jnp.float32),
        ),
        in_specs=[vmem] * 2,
        out_specs=(vmem, vmem),
        scratch_shapes=[pltpu.VMEM(shape, jnp.float32) for shape in shapes]
        + semaphores
        + column_sems(cols, 2)
        + column_sems(cols, rows),
        compiler_params=pltpu.CompilerParams(collective_id=1, has_side_effects=True, vmem_limit_bytes=48 * 1024 * 1024),
    )(panels_t, trailing)
    return r_block, spread.transpose(2, 0, 1).reshape(total // rows, -1)


def plain(panels_t, trailing_t):
    panel = lax.all_gather(panels_t, "col", axis=0, tiled=True)
    gram_part = lax.psum_scatter(product(panels_t, panel.T), "row", scatter_dimension=0, tiled=True)
    gram = lax.all_gather(gram_part, ("col", "row"), axis=0, tiled=True)
    cross = lax.psum_scatter(product(trailing_t, panel.T), "row", scatter_dimension=0, tiled=True)
    r_full, invert = factor(gram)
    slab = product(product(cross, invert.T), invert)
    return r_full, lax.all_to_all(slab, "row", split_axis=1, concat_axis=0, tiled=True).T


def local(panels_t, trailing_t):
    rows, cols = lax.axis_size("row"), lax.axis_size("col")
    width = panels_t.shape[0]
    total = width * cols
    thick = trailing_t.shape[0] // rows
    tiled = width % BLOCK == 0 and total // rows % BLOCK == 0 and width // rows % MICRO == 0 and thick % MICRO == 0
    if tiled and rows % 2 == 0 and cols % 2 == 0 and rows // 2 < total // BLOCK:
        return direct(panels_t, trailing_t, rows, cols)
    r_full, coef_block = plain(panels_t, trailing_t)
    rows_out = total // rows
    row_start = lax.axis_index("row") * rows_out
    col_start = lax.axis_index("col") * width
    r_block = lax.dynamic_slice(r_full, (row_start, col_start), (rows_out, width))
    return (r_block, coef_block)


def solution(mesh):
    placed = (P("col", "row"), P("col", "row"))
    return jax.shard_map(
        local,
        mesh=mesh,
        in_specs=placed,
        out_specs=(P("row", "col"), P("row", "col")),
        check_vma=False,
    )
```
